32 devices in a mesh: seq: 8 (over y, x, core), ch: 4 (over z).
Axes of the slice: x: 2, y: 2, z: 4, core: 2. Of those that a mesh axis runs over, the one named last changes fastest.
Arguments:
- streams: bfloat16 [3, 128, 8192], P(None, None, ('seq', 'ch')), may hold values from -6 to 6
- conv_taps: float32 [3, 128, 7], replicated, may hold values from -2.5 to 2.5
- long_filter: float32 [128, 8192], P('ch', 'seq'), may hold values from -0.06629126 to 0.06629126
- skip_gain: float32 [128], P('ch'), may hold values from -6 to 6
Outputs:
- mixer_output: bfloat16 [128, 8192], P(None, ('seq', 'ch'))
The draws below stay inside these ranges and needn't reach their ends.
All inputs are finite; a program needn't handle non-finite values.
Results may differ from the reference program's by a relative error of at most 0.0064.
Values may be sent and summed in bfloat16 or wider, within the bound.
A program may use at most 64 MiB of HBM per device.

```python
import jax
import jax.numpy as jnp

TOK_DEV = 256
TAPS = 7
CHANNELS = 128
LENGTH = 8192
N_SEQ = 8
N_CH = 4


def level_of(own_key, shape, split, low, high):
    factor_of, own = 1.0, jax.random.fold_in(own_key, 6)
    for axis_at, blocks in split:
        heights = jnp.exp(jax.random.uniform(jax.random.fold_in(own, axis_at), (blocks,), jnp.float32, low / len(split), high / len(split)))
        factor_of = factor_of * jnp.repeat(heights, shape[axis_at] // blocks).reshape([-1 if axis == axis_at else 1 for axis in range(len(shape))])
    return factor_of


def normal_values(rng, shape, deviation, most, split=(), kind=jnp.bfloat16):
    drawn = jax.random.normal(rng, shape, jnp.float32) * deviation
    if len(split) > 0:
        drawn = level_of(rng, shape, split, -0.22, 0.18) * drawn
    return jnp.clip(drawn, min=-most, max=most).astype(kind)


def setup_inputs(seed: int = 0) -> dict:
    splits = jax.random.split(jax.random.key(seed), 5)
    streams = normal_values(splits[0], (3, CHANNELS, LENGTH), 1.0, 6.0, ((2, 32),))
    conv_taps = normal_values(splits[1], (3, CHANNELS, TAPS), 0.4, 2.5, (), jnp.float32)
    long_filter = normal_values(splits[2], (CHANNELS, LENGTH), (1.0 / (TOK_DEV * N_SEQ * N_CH) ** 0.5), 0.06629126, ((0, 4), (1, 8)), jnp.float32)
    skip_gain = normal_values(splits[3], (CHANNELS,), 1.0, 6.0, ((0, 4),), jnp.float32)
    return {"streams": streams, "conv_taps": conv_taps, "long_filter": long_filter, "skip_gain": skip_gain}


def reference(streams, conv_taps, long_filter, skip_gain):
    tap_count = conv_taps.shape[2]
    length_all = streams.shape[2]
    leading = jnp.zeros(streams.shape[:2] + (tap_count - 1,), streams.dtype)
    extended = jnp.concatenate([leading, streams], axis=2).astype(jnp.float32)
    summed = jnp.zeros(streams.shape, jnp.float32)
    for offset in range(tap_count):
        begin = tap_count - 1 - offset
        summed = summed + conv_taps[:, :, offset:offset + 1] * extended[:, :, begin:begin + length_all]
    shorts = summed.astype(jnp.bfloat16)
    queries = shorts[0].astype(jnp.float32)
    product = shorts[1].astype(jnp.float32) * shorts[2].astype(jnp.float32)
    padded_len = 2 * length_all
    spectrum = jnp.fft.rfft(product, n=padded_len, axis=1) * jnp.fft.rfft(long_filter, n=padded_len, axis=1)
    longconv = jnp.fft.irfft(spectrum, n=padded_len, axis=1)[:, :length_all]
    return (queries * (longconv + skip_gain[:, None] * product)).astype(jnp.bfloat16)
```

```python
import functools
import math

import jax
import jax.numpy as jnp
from jax import lax
from jax.experimental import pallas as pl
from jax.experimental.pallas import tpu as pltpu
from jax.sharding import PartitionSpec as P

BLOCK = 64
LANES = 128
GROUP = 4
SPAN = 8


highest = lax.Precision.HIGHEST
two_pi = 2.0 * math.pi


def from_behind(value, axis, steps):
    count = lax.axis_size(axis)
    initial, last = (max(0, -steps), min(count, count - steps))
    return lax.ppermute(value, axis, [(source, source + steps) for source in range(initial, last)])


def tables(row_count, col_count, period):
    grid = lax.broadcasted_iota(jnp.int32, (row_count, col_count), 0) * lax.broadcasted_iota(
        jnp.int32, (row_count, col_count), 1
    )
    angle = (grid % period).astype(jnp.float32) * (two_pi / period)
    return (jnp.cos(angle), jnp.sin(angle))


def short_filter(block_in, upstream, weights):
    tap_count = weights.shape[2]
    extended = jnp.concatenate([upstream, block_in], axis=2).astype(jnp.float32)
    length_here = block_in.shape[2]
    summed = jnp.zeros(block_in.shape, jnp.float32)
    for offset in range(tap_count):
        begin = tap_count - 1 - offset
        summed = (
            summed
            + weights[:, :, offset : offset + 1] * extended[:, :, begin : begin + length_here]
        )
    return summed.astype(jnp.bfloat16)


def rotate(real_part, imag_part, cosine, sine):
    return (real_part * cosine + imag_part * sine, imag_part * cosine - real_part * sine)


def dft_apply(real_part, imag_part, form, cosine, sine):
    first = jnp.einsum(form, real_part, cosine, precision=highest) + jnp.einsum(
        form, imag_part, sine, precision=highest
    )
    second = jnp.einsum(form, imag_part, cosine, precision=highest) - jnp.einsum(
        form, real_part, sine, precision=highest
    )
    return (first, second)


def section_one(moved, cos_seq, sin_seq, total_items, columns_each):
    family = moved.shape[0]
    real_part = jnp.einsum("fcst,sk->fckt", moved, cos_seq, precision=highest)
    imag_part = -jnp.einsum("fcst,sk->fckt", moved, sin_seq, precision=highest)
    return jnp.stack([real_part, imag_part]).reshape(2, family, total_items, columns_each)


def local(streams, conv_taps, long_filter, skip_gain):
    seq_count = lax.axis_size("seq")
    seq_pos = lax.axis_index("seq")
    group_pos = lax.axis_index("ch")
    channels = long_filter.shape[0]
    tokens_here = long_filter.shape[1]
    tap_count = conv_taps.shape[2]
    length = tokens_here * seq_count
    padded_len = 2 * length
    columns_each = tokens_here // seq_count
    doubled = 2 * seq_count
    item_count = channels * doubled // seq_count
    total_items = channels * doubled
    inner_len = tokens_here // BLOCK
    cos_seq, sin_seq = tables(seq_count, doubled, doubled)
    regrouped = lax.all_to_all(streams, "ch", split_axis=1, concat_axis=2, tiled=True)
    upstream = from_behind(regrouped[:, :, regrouped.shape[2] - (tap_count - 1) :], "seq", 1)
    own_taps = lax.dynamic_slice_in_dim(conv_taps, group_pos * channels, channels, 1)
    shorts = short_filter(regrouped, upstream, own_taps)
    queries = shorts[0].astype(jnp.float32)
    product = shorts[1].astype(jnp.float32) * shorts[2].astype(jnp.float32)
    both_moved = lax.all_to_all(
        jnp.stack([product, long_filter]).reshape(2, channels, 1, tokens_here),
        "seq",
        split_axis=3,
        concat_axis=2,
        tiled=True,
    )
    spectra_rows = lax.all_to_all(
        section_one(both_moved, cos_seq, sin_seq, total_items, columns_each),
        "seq",
        split_axis=2,
        concat_axis=3,
        tiled=True,
    )
    z_real = spectra_rows[0]
    z_imag = spectra_rows[1]
    cos_outer, sin_outer = tables(BLOCK, BLOCK, BLOCK)
    cos_inner, sin_inner = tables(inner_len, inner_len, inner_len)
    cos_mid, sin_mid = tables(BLOCK, inner_len, tokens_here)
    global_item = seq_pos * item_count + lax.iota(jnp.int32, item_count)
    freq = global_item % doubled
    twiddle_grid = lax.iota(jnp.int32, tokens_here)[None, :] * freq[:, None] % padded_len
    twiddle_angle = twiddle_grid.astype(jnp.float32) * (two_pi / padded_len)
    cos_twiddle = jnp.cos(twiddle_angle)
    sin_twiddle = jnp.sin(twiddle_angle)
    z_real, z_imag = rotate(z_real, z_imag, cos_twiddle, sin_twiddle)
    family = z_real.shape[0]
    z_real = z_real.reshape(family, item_count, BLOCK, inner_len)
    z_imag = z_imag.reshape(family, item_count, BLOCK, inner_len)
    z_real, z_imag = dft_apply(z_real, z_imag, "fiab,ae->fieb", cos_outer, sin_outer)
    z_real, z_imag = rotate(z_real, z_imag, cos_mid, sin_mid)
    z_real, z_imag = dft_apply(z_real, z_imag, "fieb,bg->fieg", cos_inner, sin_inner)
    prod_real = z_real[0] * z_real[1] - z_imag[0] * z_imag[1]
    prod_imag = z_real[0] * z_imag[1] + z_imag[0] * z_real[1]
    prod_real, prod_imag = dft_apply(prod_real, prod_imag, "ieg,gb->ieb", cos_inner, -sin_inner)
    prod_real, prod_imag = rotate(prod_real, prod_imag, cos_mid, -sin_mid)
    prod_real, prod_imag = dft_apply(prod_real, prod_imag, "ieb,ea->iab", cos_outer, -sin_outer)
    prod_real = prod_real.reshape(item_count, tokens_here)
    prod_imag = prod_imag.reshape(item_count, tokens_here)
    prod_real, prod_imag = rotate(prod_real, prod_imag, cos_twiddle, -sin_twiddle)
    returned = lax.all_to_all(
        jnp.stack([prod_real, prod_imag]), "seq", split_axis=2, concat_axis=1, tiled=True
    )
    returned = returned.reshape(2, channels, doubled, columns_each)
    partial_out = jnp.einsum("ckt,sk->cst", returned[0], cos_seq, precision=highest) - jnp.einsum(
        "ckt,sk->cst", returned[1], sin_seq, precision=highest
    )
    partial_out = partial_out * (1.0 / padded_len)
    longconv = lax.all_to_all(partial_out, "seq", split_axis=1, concat_axis=2, tiled=True).reshape(
        channels, tokens_here
    )
    gated = (queries * (longconv + skip_gain[:, None] * product)).astype(jnp.bfloat16)
    return lax.all_to_all(gated, "ch", split_axis=1, concat_axis=0, tiled=True)

MESH = pl.DeviceIdType.MESH


def owner_kernel(
    seq_count,
    ch_count,
    tap_count,
    streams,
    filt,
    aux,
    out,
    send_x,
    send_f,
    got_x,
    got_f,
    rows,
    done,
    send_o,
    got_o,
    wheel,
    x_send,
    x_recv,
    f_send,
    f_recv,
    o_send,
    o_recv,
):
    count = seq_count * ch_count
    seq_pos, ch_pos = lax.axis_index("seq"), lax.axis_index("ch")
    me = seq_pos * ch_count + ch_pos
    mine = ch_pos * seq_count + seq_pos
    width = streams.shape[2]
    span_f = filt.shape[1]
    blocks = width * count // LANES
    halves = width // LANES
    base = 8 * blocks

    def peer(step):
        other = lax.rem(me + step, count)
        return other, other // ch_count, lax.rem(other, ch_count)

    barrier = pltpu.get_barrier_semaphore()

    @pl.loop(1, count)
    def _(step):
        _, s, c = peer(step)
        pl.semaphore_signal(barrier, inc=1, device_id=(s, c), device_id_type=MESH)

    for s in range(seq_count):
        send_f[s] = filt[GROUP * s : GROUP * (s + 1), :]

    @pl.loop(0, streams.shape[1] // 16)
    def _(m):
        at = pl.ds(pl.multiple_of(16 * m, 16), 16)
        q, k, v = [streams[i, at, :].astype(jnp.float32) for i in range(3)]
        for e in range(4):
            part = slice(4 * e, 4 * e + 4)
            send_x[4 * m + e] = jnp.concatenate([q[part], k[part], v[part], v[part]], axis=0).astype(jnp.bfloat16)

    pl.semaphore_wait(barrier, count - 1)

    def filter_copy(s_to, s_from):
        at = pl.ds(pl.multiple_of(s_from * span_f, LANES), span_f)
        return pltpu.make_async_remote_copy(
            src_ref=send_f.at[s_to],
            dst_ref=got_f.at[:, at],
            send_sem=f_send.at[s_to],
            recv_sem=f_recv.at[s_from],
            device_id=(s_to, ch_pos),
            device_id_type=MESH,
        )

    def stream_copy(other, s, c, source):
        at = pl.ds(pl.multiple_of(LANES + source * width, LANES), width)
        block = c * seq_count + s
        return pltpu.make_async_remote_copy(
            src_ref=send_x.at[block],
            dst_ref=got_x.at[:, at],
            send_sem=x_send.at[other],
            recv_sem=x_recv.at[source],
            device_id=(s, c),
            device_id_type=MESH,
        )

    def out_copy(other, s, c, source):
        return pltpu.make_async_remote_copy(
            src_ref=send_o.at[other],
            dst_ref=got_o.at[source],
            send_sem=o_send.at[other],
            recv_sem=o_recv.at[source],
            device_id=(s, c),
            device_id_type=MESH,
        )

    @pl.loop(1, seq_count)
    def _(step):
        filter_copy(lax.rem(seq_pos + step, seq_count), seq_pos).start()

    @pl.loop(1, count)
    def _(step):
        other, s, c = peer(step)
        stream_copy(other, s, c, me).start()

    got_f[:, pl.ds(pl.multiple_of(seq_pos * span_f, LANES), span_f)] = send_f[seq_pos]
    got_x[:, pl.ds(pl.multiple_of(LANES + me * width, LANES), width)] = send_x[mine]
    got_x[:, 0:LANES] = jnp.zeros((16, LANES), jnp.bfloat16)
    rows[0:base, :] = jnp.zeros((base, LANES), jnp.float32)

    @pl.loop(1, seq_count)
    def _(step):
        filter_copy(lax.rem(seq_pos + step, seq_count), lax.rem(seq_pos + step, seq_count)).wait_recv()

    @pl.loop(1, count)
    def _(step):
        other, s, c = peer(step)
        stream_copy(other, s, c, other).wait_recv()

    chunk = 4 * LANES
    taps = [jnp.concatenate([aux[j]] * 4, axis=1) for j in range(tap_count)]

    @pl.loop(0, blocks // 4)
    def _(i):
        ext = got_x[:, pl.ds(pl.multiple_of(i * chunk, LANES), chunk + LANES)].astype(jnp.float32)
        total = taps[0] * ext[:, LANES:]
        for j in range(1, tap_count):
            total = total + taps[j] * pltpu.roll(ext, j, 1)[:, LANES:]
        shorts = total.astype(jnp.bfloat16).astype(jnp.float32)
        product = shorts[4:8] * shorts[8:12]
        both = jnp.concatenate([product, shorts[0:4]], axis=0)
        for u in range(4):
            rows[pl.ds(pl.multiple_of(base + 8 * (4 * i + u), 8), 8), :] = both[:, LANES * u : LANES * (u + 1)]

    row_at = lax.broadcasted_iota(jnp.int32, (LANES, LANES), 0)
    lane_at = lax.broadcasted_iota(jnp.int32, (LANES, LANES), 1)
    upper = lane_at >= row_at

    for c in range(GROUP):
        wheel[...] = jnp.zeros_like(wheel)

        def body(big, total):
            last = wheel[...]
            lags, shifted = [], []
            for u in range(SPAN):
                d = big * SPAN + u
                h = got_f[c : c + 1, pl.ds(pl.multiple_of(d * LANES, LANES), LANES)]
                turn = pltpu.roll(jnp.broadcast_to(h, (LANES, LANES)), 0, 1, stride=1, stride_axis=0)
                lags.append(jnp.where(upper, turn, last).astype(jnp.bfloat16))
                shifted.append(rows[pl.ds(base + c - 8 * d, blocks, stride=8), :].astype(jnp.bfloat16))
                last = turn
            wheel[...] = last
            return total + jnp.dot(
                jnp.concatenate(shifted, axis=1),
                jnp.concatenate(lags, axis=0),
                preferred_element_type=jnp.float32,
            )

        conv = lax.fori_loop(0, blocks // SPAN, body, jnp.zeros((blocks, LANES), jnp.float32))
        product = rows[pl.ds(base + c, blocks, stride=8), :]
        q = rows[pl.ds(base + GROUP + c, blocks, stride=8), :]
        gain = aux[tap_count, c : c + 1, :]
        done[pl.ds(c, blocks, stride=GROUP), :] = q * (conv + gain * product)

    @pl.loop(0, count)
    def _(t):
        send_o[t] = done[pl.ds(pl.multiple_of(8 * t, 8), 8), :].astype(send_o.dtype)

    @pl.loop(1, count)
    def _(step):
        other, s, c = peer(step)
        out_copy(other, s, c, mine).start()

    got_o[mine] = send_o[me]

    @pl.loop(1, count)
    def _(step):
        other, s, c = peer(step)
        out_copy(other, s, c, c * seq_count + s).wait_recv()

    @pl.loop(0, count // 4)
    def _(m):
        parts = [got_o[4 * m + e].astype(jnp.float32) for e in range(4)]
        at = pl.ds(pl.multiple_of(16 * m, 16), 16)
        for half in range(2):
            piece = jnp.concatenate([p[4 * half : 4 * half + 4] for p in parts], axis=0)
            out[at, LANES * half : LANES * (half + 1)] = piece.astype(jnp.bfloat16)

    @pl.loop(1, seq_count)
    def _(step):
        filter_copy(lax.rem(seq_pos + step, seq_count), seq_pos).wait_send()

    @pl.loop(1, count)
    def _(step):
        other, s, c = peer(step)
        stream_copy(other, s, c, me).wait_send()
        out_copy(other, s, c, mine).wait_send()


def owner_local(streams, conv_taps, long_filter, skip_gain):
    seq_count, ch_count = lax.axis_size("seq"), lax.axis_size("ch")
    seq_pos, ch_pos = lax.axis_index("seq"), lax.axis_index("ch")
    count = seq_count * ch_count
    channels, width = streams.shape[1:]
    tap_count = conv_taps.shape[2]
    length = width * count
    mine = ch_pos * seq_count + seq_pos
    own_taps = lax.dynamic_slice_in_dim(conv_taps, mine * GROUP, GROUP, 1).reshape(3 * GROUP, tap_count)
    own_taps = jnp.pad(own_taps.T, ((0, 0), (0, GROUP)))
    own_gain = jnp.pad(lax.dynamic_slice_in_dim(skip_gain, seq_pos * GROUP, GROUP, 0), (0, 3 * GROUP))
    aux = jnp.concatenate([own_taps, own_gain[None]], axis=0)
    aux = jnp.broadcast_to(aux[:, :, None], aux.shape + (LANES,))
    blocks = length // LANES
    dma = pltpu.SemaphoreType.DMA
    return pl.pallas_call(
        functools.partial(owner_kernel, seq_count, ch_count, tap_count),
        out_shape=jax.ShapeDtypeStruct((channels, width), jnp.bfloat16),
        in_specs=[pl.BlockSpec(memory_space=pltpu.VMEM)] * 3,
        out_specs=pl.BlockSpec(memory_space=pltpu.VMEM),
        scratch_shapes=[
            pltpu.VMEM((count, 16, width), jnp.bfloat16),
            pltpu.VMEM((seq_count, GROUP, long_filter.shape[1]), jnp.float32),
            pltpu.VMEM((16, LANES + length), jnp.bfloat16),
            pltpu.VMEM((GROUP, length), jnp.float32),
            pltpu.VMEM((16 * blocks, LANES), jnp.float32),
            pltpu.VMEM((GROUP * blocks, LANES), jnp.float32),
            pltpu.VMEM((count, 8, LANES), jnp.bfloat16),
            pltpu.VMEM((count, 8, LANES), jnp.bfloat16),
            pltpu.VMEM((LANES, LANES), jnp.float32),
            dma((count,)),
            dma((count,)),
            dma((seq_count,)),
            dma((seq_count,)),
            dma((count,)),
            dma((count,)),
        ],
        compiler_params=pltpu.CompilerParams(
            collective_id=0, has_side_effects=True, vmem_limit_bytes=32 * 1024 * 1024
        ),
    )(streams, long_filter, aux)


def pick(streams, conv_taps, long_filter, skip_gain):
    count = lax.axis_size("seq") * lax.axis_size("ch")
    fits = streams.shape[1] == GROUP * count and streams.shape[2] == 2 * LANES and count % 4 == 0
    return (owner_local if fits else local)(streams, conv_taps, long_filter, skip_gain)


def solution(mesh):
    return jax.shard_map(
        pick,
        mesh=mesh,
        in_specs=(P(None, None, ("seq", "ch")), P(), P("ch", "seq"), P("ch")),
        out_specs=P(None, ("seq", "ch")),
        check_vma=False,
    )
```

```python
import functools
import math

import jax
import jax.numpy as jnp
from jax import lax
from jax.experimental import pallas as pl
from jax.experimental.pallas import tpu as pltpu
from jax.sharding import PartitionSpec as P

BLOCK = 64
LANES = 128
GROUP = 4
SPAN = 8


highest = lax.Precision.HIGHEST
two_pi = 2.0 * math.pi


def from_behind(value, axis, steps):
    count = lax.axis_size(axis)
    initial, last = (max(0, -steps), min(count, count - steps))
    return lax.ppermute(value, axis, [(source, source + steps) for source in range(initial, last)])


def tables(row_count, col_count, period):
    grid = lax.broadcasted_iota(jnp.int32, (row_count, col_count), 0) * lax.broadcasted_iota(
        jnp.int32, (row_count, col_count), 1
    )
    angle = (grid % period).astype(jnp.float32) * (two_pi / period)
    return (jnp.cos(angle), jnp.sin(angle))


def short_filter(block_in, upstream, weights):
    tap_count = weights.shape[2]
    extended = jnp.concatenate([upstream, block_in], axis=2).astype(jnp.float32)
    length_here = block_in.shape[2]
    summed = jnp.zeros(block_in.shape, jnp.float32)
    for offset in range(tap_count):
        begin = tap_count - 1 - offset
        summed = (
            summed
            + weights[:, :, offset : offset + 1] * extended[:, :, begin : begin + length_here]
        )
    return summed.astype(jnp.bfloat16)


def rotate(real_part, imag_part, cosine, sine):
    return (real_part * cosine + imag_part * sine, imag_part * cosine - real_part * sine)


def dft_apply(real_part, imag_part, form, cosine, sine):
    first = jnp.einsum(form, real_part, cosine, precision=highest) + jnp.einsum(
        form, imag_part, sine, precision=highest
    )
    second = jnp.einsum(form, imag_part, cosine, precision=highest) - jnp.einsum(
        form, real_part, sine, precision=highest
    )
    return (first, second)


def section_one(moved, cos_seq, sin_seq, total_items, columns_each):
    family = moved.shape[0]
    real_part = jnp.einsum("fcst,sk->fckt", moved, cos_seq, precision=highest)
    imag_part = -jnp.einsum("fcst,sk->fckt", moved, sin_seq, precision=highest)
    return jnp.stack([real_part, imag_part]).reshape(2, family, total_items, columns_each)


def local(streams, conv_taps, long_filter, skip_gain):
    seq_count = lax.axis_size("seq")
    seq_pos = lax.axis_index("seq")
    group_pos = lax.axis_index("ch")
    channels = long_filter.shape[0]
    tokens_here = long_filter.shape[1]
    tap_count = conv_taps.shape[2]
    length = tokens_here * seq_count
    padded_len = 2 * length
    columns_each = tokens_here // seq_count
    doubled = 2 * seq_count
    item_count = channels * doubled // seq_count
    total_items = channels * doubled
    inner_len = tokens_here // BLOCK
    cos_seq, sin_seq = tables(seq_count, doubled, doubled)
    regrouped = lax.all_to_all(streams, "ch", split_axis=1, concat_axis=2, tiled=True)
    upstream = from_behind(regrouped[:, :, regrouped.shape[2] - (tap_count - 1) :], "seq", 1)
    own_taps = lax.dynamic_slice_in_dim(conv_taps, group_pos * channels, channels, 1)
    shorts = short_filter(regrouped, upstream, own_taps)
    queries = shorts[0].astype(jnp.float32)
    product = shorts[1].astype(jnp.float32) * shorts[2].astype(jnp.float32)
    both_moved = lax.all_to_all(
        jnp.stack([product, long_filter]).reshape(2, channels, 1, tokens_here),
        "seq",
        split_axis=3,
        concat_axis=2,
        tiled=True,
    )
    spectra_rows = lax.all_to_all(
        section_one(both_moved, cos_seq, sin_seq, total_items, columns_each),
        "seq",
        split_axis=2,
        concat_axis=3,
        tiled=True,
    )
    z_real = spectra_rows[0]
    z_imag = spectra_rows[1]
    cos_outer, sin_outer = tables(BLOCK, BLOCK, BLOCK)
    cos_inner, sin_inner = tables(inner_len, inner_len, inner_len)
    cos_mid, sin_mid = tables(BLOCK, inner_len, tokens_here)
    global_item = seq_pos * item_count + lax.iota(jnp.int32, item_count)
    freq = global_item % doubled
    twiddle_grid = lax.iota(jnp.int32, tokens_here)[None, :] * freq[:, None] % padded_len
    twiddle_angle = twiddle_grid.astype(jnp.float32) * (two_pi / padded_len)
    cos_twiddle = jnp.cos(twiddle_angle)
    sin_twiddle = jnp.sin(twiddle_angle)
    z_real, z_imag = rotate(z_real, z_imag, cos_twiddle, sin_twiddle)
    family = z_real.shape[0]
    z_real = z_real.reshape(family, item_count, BLOCK, inner_len)
    z_imag = z_imag.reshape(family, item_count, BLOCK, inner_len)
    z_real, z_imag = dft_apply(z_real, z_imag, "fiab,ae->fieb", cos_outer, sin_outer)
    z_real, z_imag = rotate(z_real, z_imag, cos_mid, sin_mid)
    z_real, z_imag = dft_apply(z_real, z_imag, "fieb,bg->fieg", cos_inner, sin_inner)
    prod_real = z_real[0] * z_real[1] - z_imag[0] * z_imag[1]
    prod_imag = z_real[0] * z_imag[1] + z_imag[0] * z_real[1]
    prod_real, prod_imag = dft_apply(prod_real, prod_imag, "ieg,gb->ieb", cos_inner, -sin_inner)
    prod_real, prod_imag = rotate(prod_real, prod_imag, cos_mid, -sin_mid)
    prod_real, prod_imag = dft_apply(prod_real, prod_imag, "ieb,ea->iab", cos_outer, -sin_outer)
    prod_real = prod_real.reshape(item_count, tokens_here)
    prod_imag = prod_imag.reshape(item_count, tokens_here)
    prod_real, prod_imag = rotate(prod_real, prod_imag, cos_twiddle, -sin_twiddle)
    returned = lax.all_to_all(
        jnp.stack([prod_real, prod_imag]), "seq", split_axis=2, concat_axis=1, tiled=True
    )
    returned = returned.reshape(2, channels, doubled, columns_each)
    partial_out = jnp.einsum("ckt,sk->cst", returned[0], cos_seq, precision=highest) - jnp.einsum(
        "ckt,sk->cst", returned[1], sin_seq, precision=highest
    )
    partial_out = partial_out * (1.0 / padded_len)
    longconv = lax.all_to_all(partial_out, "seq", split_axis=1, concat_axis=2, tiled=True).reshape(
        channels, tokens_here
    )
    gated = (queries * (longconv + skip_gain[:, None] * product)).astype(jnp.bfloat16)
    return lax.all_to_all(gated, "ch", split_axis=1, concat_axis=0, tiled=True)

MESH = pl.DeviceIdType.MESH


def owner_kernel(
    seq_count,
    ch_count,
    streams_in,
    filt_in,
    taps_in,
    gains_in,
    out,
    streams,
    filt,
    send_x,
    send_f,
    got_x,
    got_f,
    tap_rows,
    rows,
    lags,
    done,
    part,
    send_o,
    got_o,
    load_sem,
    x_send,
    x_recv,
    f_send,
    f_recv,
    o_send,
    o_recv,
):
    count = seq_count * ch_count
    seq_pos, ch_pos = lax.axis_index("seq"), lax.axis_index("ch")
    me = seq_pos * ch_count + ch_pos
    mine = ch_pos * seq_count + seq_pos
    width = streams.shape[2]
    span_f = filt.shape[1]
    tap_count = taps_in.shape[1]
    blocks = width * count // LANES
    half = blocks // 2
    base = 8 * blocks
    f32, bf16 = jnp.float32, jnp.bfloat16

    def peer(step):
        other = lax.rem(me + step, count)
        return other, other // ch_count, lax.rem(other, ch_count)

    barrier = pltpu.get_barrier_semaphore()

    @pl.loop(1, count)
    def _(step):
        _, s, c = peer(step)
        pl.semaphore_signal(barrier, inc=1, device_id=(s, c), device_id_type=MESH)

    load_f = pltpu.make_async_copy(filt_in, filt, load_sem.at[0])
    load_x = pltpu.make_async_copy(streams_in, streams, load_sem.at[1])
    load_f.start()
    load_x.start()
    lane = lax.broadcasted_iota(jnp.int32, (tap_count, LANES), 1)
    for c in range(GROUP):
        for i in range(3):
            column = jnp.sum(jnp.where(lane == GROUP * mine + c, taps_in[i], 0.0), axis=1, keepdims=True)
            tap_rows[pl.ds(32 * i + c, tap_count, stride=GROUP), :] = jnp.broadcast_to(column, (tap_count, LANES))
    rows[0:base, :] = jnp.zeros((base, LANES), f32)
    for i in range(3):
        got_x[i, :, 0:LANES] = jnp.zeros((GROUP, LANES), bf16)
    got_f[:, 0:LANES] = jnp.zeros((GROUP, LANES), bf16)

    load_f.wait()
    for s in range(seq_count):
        send_f[s] = filt[GROUP * s : GROUP * (s + 1), :].astype(bf16)
    load_x.wait()

    @pl.loop(0, streams.shape[1] // 16)
    def _(m):
        at = pl.ds(pl.multiple_of(16 * m, 16), 16)
        for i in range(3):
            values = streams[i, at, :].astype(f32)
            for e in range(4):
                send_x[4 * m + e, i] = values[4 * e : 4 * e + 4].astype(bf16)

    pl.semaphore_wait(barrier, count - 1)

    def filter_copy(s_to, s_from):
        at = pl.ds(pl.multiple_of(LANES + s_from * span_f, LANES), span_f)
        return pltpu.make_async_remote_copy(
            src_ref=send_f.at[s_to],
            dst_ref=got_f.at[:, at],
            send_sem=f_send.at[s_to],
            recv_sem=f_recv.at[s_from],
            device_id=(s_to, ch_pos),
            device_id_type=MESH,
        )

    def stream_copy(other, s, c, source):
        at = pl.ds(pl.multiple_of(LANES + source * width, LANES), width)
        block = c * seq_count + s
        return pltpu.make_async_remote_copy(
            src_ref=send_x.at[block],
            dst_ref=got_x.at[:, :, at],
            send_sem=x_send.at[other],
            recv_sem=x_recv.at[source],
            device_id=(s, c),
            device_id_type=MESH,
        )

    def out_copy(other, source):
        return pltpu.make_async_remote_copy(
            src_ref=send_o.at[other],
            dst_ref=got_o.at[source],
            send_sem=o_send.at[other],
            recv_sem=o_recv.at[source],
            device_id=(other // ch_count, lax.rem(other, ch_count)),
            device_id_type=MESH,
        )

    @pl.loop(1, seq_count)
    def _(step):
        filter_copy(lax.rem(seq_pos + step, seq_count), seq_pos).start()

    @pl.loop(1, count)
    def _(step):
        other, s, c = peer(step)
        stream_copy(other, s, c, me).start()

    got_f[:, pl.ds(pl.multiple_of(LANES + seq_pos * span_f, LANES), span_f)] = send_f[seq_pos]
    for i in range(3):
        got_x[i, :, pl.ds(pl.multiple_of(LANES + me * width, LANES), width)] = send_x[mine, i]

    @pl.loop(1, seq_count)
    def _(step):
        source = lax.rem(seq_pos + step, seq_count)
        filter_copy(source, source).wait_recv()

    row_at = lax.broadcasted_iota(jnp.int32, (LANES, LANES), 0)
    lane_at = lax.broadcasted_iota(jnp.int32, (LANES, LANES), 1)
    upper = lane_at >= row_at

    @pl.loop(0, blocks // SPAN)
    def _(big):
        wide = SPAN * LANES
        window = got_f[:, pl.ds(pl.multiple_of(big * wide, LANES), wide + LANES)].astype(f32)
        for c in range(GROUP):
            last = None
            for u in range(SPAN + 1):
                h = jnp.broadcast_to(window[c : c + 1, LANES * u : LANES * (u + 1)], (LANES, LANES))
                turn = pltpu.roll(h, 0, 1, stride=1, stride_axis=0)
                if u > 0:
                    at = pl.ds(pl.multiple_of((big * SPAN + u - 1) * LANES, LANES), LANES)
                    lags[c, at, :] = jnp.where(upper, turn, last).astype(bf16)
                last = turn

    chunk = 4 * LANES
    taps = []
    for j in range(tap_count):
        r = [tap_rows[32 * i + GROUP * j : 32 * i + GROUP * j + GROUP, :] for i in range(3)]
        qk = jnp.concatenate(r[:2], axis=0)
        taps.append([jnp.concatenate([t] * 4, axis=1) for t in (qk, r[2])])

    @pl.loop(0, blocks // 4)
    def _(n):
        for e in range(2):
            source = 2 * n + e

            @pl.when(source != me)
            def _():
                stream_copy(source, source // ch_count, lax.rem(source, ch_count), source).wait_recv()

        at = pl.ds(pl.multiple_of(n * chunk, LANES), chunk + LANES)
        q, k, v = [got_x[i, :, at].astype(f32) for i in range(3)]
        shorts = []
        for which, ext in enumerate((jnp.concatenate([q, k], axis=0), v)):
            total = taps[0][which] * ext[:, LANES:]
            for j in range(1, tap_count):
                total = total + taps[j][which] * pltpu.roll(ext, j, 1)[:, LANES:]
            shorts.append(total.astype(bf16).astype(f32))
        product = shorts[0][GROUP:] * shorts[1]
        both = jnp.concatenate([product, shorts[0][:GROUP]], axis=0)
        for u in range(4):
            rows[pl.ds(pl.multiple_of(base + 8 * (4 * n + u), 8), 8), :] = both[:, LANES * u : LANES * (u + 1)]

    gain_lane = lax.broadcasted_iota(jnp.int32, gains_in.shape, 1)

    def partial_conv(c, first, many, d_from):
        at = [pl.ds(base + c + 8 * (first - d), many, stride=8) for d in range(d_from, d_from + half)]
        shifted = jnp.concatenate([rows[a, :].astype(bf16) for a in at], axis=1)
        return jnp.dot(shifted, lags[c, LANES * d_from : LANES * (d_from + half), :], preferred_element_type=f32)

    def finish(c, first, conv):
        product = rows[pl.ds(base + 8 * first + c, half, stride=8), :]
        q = rows[pl.ds(base + 8 * first + GROUP + c, half, stride=8), :]
        gain = jnp.sum(jnp.where(gain_lane == GROUP * seq_pos + c, gains_in[...], 0.0), axis=1, keepdims=True)
        done[pl.ds(GROUP * first + c, half, stride=GROUP), :] = q * (conv + gain * product)

    def send_half(first):
        for t in range(first, first + count // 2):
            send_o[t] = done[8 * t : 8 * t + 8, :].astype(bf16)

        @pl.loop(0, count // 2)
        def _(step):
            other = first + lax.rem(me + step, count // 2)

            @pl.when(other != me)
            def _():
                out_copy(other, mine).start()

    for c in range(GROUP):
        conv = partial_conv(c, 0, blocks, 0)
        finish(c, 0, conv[:half])
        part[c] = conv[half:]
    send_half(0)
    for c in range(GROUP):
        finish(c, half, part[c] + partial_conv(c, half, half, half))
    send_half(count // 2)

    got_o[mine] = send_o[me]

    @pl.loop(1, seq_count)
    def _(step):
        filter_copy(lax.rem(seq_pos + step, seq_count), seq_pos).wait_send()

    @pl.loop(1, count)
    def _(step):
        other, s, c = peer(step)
        stream_copy(other, s, c, me).wait_send()

    @pl.loop(1, count)
    def _(step):
        other, s, c = peer(step)
        out_copy(other, c * seq_count + s).wait_recv()

    @pl.loop(0, count // 4)
    def _(m):
        parts = [got_o[4 * m + e].astype(f32) for e in range(4)]
        at = pl.ds(pl.multiple_of(16 * m, 16), 16)
        for side in range(2):
            piece = jnp.concatenate([p[4 * side : 4 * side + 4] for p in parts], axis=0)
            out[at, LANES * side : LANES * (side + 1)] = piece.astype(bf16)

    @pl.loop(1, count)
    def _(step):
        out_copy(lax.rem(me + step, count), mine).wait_send()


def owner_local(streams, conv_taps, long_filter, skip_gain):
    seq_count, ch_count = lax.axis_size("seq"), lax.axis_size("ch")
    count = seq_count * ch_count
    channels, width = streams.shape[1:]
    length = width * count
    blocks = length // LANES
    dma = pltpu.SemaphoreType.DMA
    f32, bf16 = jnp.float32, jnp.bfloat16
    anywhere = pl.BlockSpec(memory_space=pl.ANY)
    inside = pl.BlockSpec(memory_space=pltpu.VMEM)
    return pl.pallas_call(
        functools.partial(owner_kernel, seq_count, ch_count),
        out_shape=jax.ShapeDtypeStruct((channels, width), bf16),
        in_specs=[anywhere, anywhere, inside, inside],
        out_specs=inside,
        scratch_shapes=[
            pltpu.VMEM(streams.shape, bf16),
            pltpu.VMEM(long_filter.shape, f32),
            pltpu.VMEM((count, 3, GROUP, width), bf16),
            pltpu.VMEM((seq_count, GROUP, long_filter.shape[1]), bf16),
            pltpu.VMEM((3, GROUP, LANES + length), bf16),
            pltpu.VMEM((GROUP, LANES + length), bf16),
            pltpu.VMEM((96, LANES), f32),
            pltpu.VMEM((16 * blocks, LANES), f32),
            pltpu.VMEM((GROUP, length, LANES), bf16),
            pltpu.VMEM((GROUP * blocks, LANES), f32),
            pltpu.VMEM((GROUP, blocks // 2, LANES), f32),
            pltpu.VMEM((count, 8, LANES), bf16),
            pltpu.VMEM((count, 8, LANES), bf16),
            dma((2,)),
            dma((count,)),
            dma((count,)),
            dma((seq_count,)),
            dma((seq_count,)),
            dma((count,)),
            dma((count,)),
        ],
        compiler_params=pltpu.CompilerParams(
            collective_id=0, has_side_effects=True, vmem_limit_bytes=48 * 1024 * 1024
        ),
    )(streams, long_filter, jnp.swapaxes(conv_taps, 1, 2), skip_gain[None, :])


def pick(streams, conv_taps, long_filter, skip_gain):
    count = lax.axis_size("seq") * lax.axis_size("ch")
    tap_fit = conv_taps.shape[2] <= 8
    tokens_fit = streams.shape[2] == 2 * LANES and streams.shape[1] == LANES
    fits = streams.shape[1] == GROUP * count and tokens_fit and tap_fit
    return (owner_local if fits else local)(streams, conv_taps, long_filter, skip_gain)


def solution(mesh):
    return jax.shard_map(
        pick,
        mesh=mesh,
        in_specs=(P(None, None, ("seq", "ch")), P(), P("ch", "seq"), P("ch")),
        out_specs=P(None, ("seq", "ch")),
        check_vma=False,
    )
```

```python
import functools
import math

import jax
import jax.numpy as jnp
from jax import lax
from jax.experimental import pallas as pl
from jax.experimental.pallas import tpu as pltpu
from jax.sharding import PartitionSpec as P

BLOCK = 64
LANES = 128
GROUP = 4
SPAN = 8


highest = lax.Precision.HIGHEST
two_pi = 2.0 * math.pi


def from_behind(value, axis, steps):
    count = lax.axis_size(axis)
    initial, last = (max(0, -steps), min(count, count - steps))
    return lax.ppermute(value, axis, [(source, source + steps) for source in range(initial, last)])


def tables(row_count, col_count, period):
    grid = lax.broadcasted_iota(jnp.int32, (row_count, col_count), 0) * lax.broadcasted_iota(
        jnp.int32, (row_count, col_count), 1
    )
    angle = (grid % period).astype(jnp.float32) * (two_pi / period)
    return (jnp.cos(angle), jnp.sin(angle))


def short_filter(block_in, upstream, weights):
    tap_count = weights.shape[2]
    extended = jnp.concatenate([upstream, block_in], axis=2).astype(jnp.float32)
    length_here = block_in.shape[2]
    summed = jnp.zeros(block_in.shape, jnp.float32)
    for offset in range(tap_count):
        begin = tap_count - 1 - offset
        summed = (
            summed
            + weights[:, :, offset : offset + 1] * extended[:, :, begin : begin + length_here]
        )
    return summed.astype(jnp.bfloat16)


def rotate(real_part, imag_part, cosine, sine):
    return (real_part * cosine + imag_part * sine, imag_part * cosine - real_part * sine)


def dft_apply(real_part, imag_part, form, cosine, sine):
    first = jnp.einsum(form, real_part, cosine, precision=highest) + jnp.einsum(
        form, imag_part, sine, precision=highest
    )
    second = jnp.einsum(form, imag_part, cosine, precision=highest) - jnp.einsum(
        form, real_part, sine, precision=highest
    )
    return (first, second)


def section_one(moved, cos_seq, sin_seq, total_items, columns_each):
    family = moved.shape[0]
    real_part = jnp.einsum("fcst,sk->fckt", moved, cos_seq, precision=highest)
    imag_part = -jnp.einsum("fcst,sk->fckt", moved, sin_seq, precision=highest)
    return jnp.stack([real_part, imag_part]).reshape(2, family, total_items, columns_each)


def local(streams, conv_taps, long_filter, skip_gain):
    seq_count = lax.axis_size("seq")
    seq_pos = lax.axis_index("seq")
    group_pos = lax.axis_index("ch")
    channels = long_filter.shape[0]
    tokens_here = long_filter.shape[1]
    tap_count = conv_taps.shape[2]
    length = tokens_here * seq_count
    padded_len = 2 * length
    columns_each = tokens_here // seq_count
    doubled = 2 * seq_count
    item_count = channels * doubled // seq_count
    total_items = channels * doubled
    inner_len = tokens_here // BLOCK
    cos_seq, sin_seq = tables(seq_count, doubled, doubled)
    regrouped = lax.all_to_all(streams, "ch", split_axis=1, concat_axis=2, tiled=True)
    upstream = from_behind(regrouped[:, :, regrouped.shape[2] - (tap_count - 1) :], "seq", 1)
    own_taps = lax.dynamic_slice_in_dim(conv_taps, group_pos * channels, channels, 1)
    shorts = short_filter(regrouped, upstream, own_taps)
    queries = shorts[0].astype(jnp.float32)
    product = shorts[1].astype(jnp.float32) * shorts[2].astype(jnp.float32)
    both_moved = lax.all_to_all(
        jnp.stack([product, long_filter]).reshape(2, channels, 1, tokens_here),
        "seq",
        split_axis=3,
        concat_axis=2,
        tiled=True,
    )
    spectra_rows = lax.all_to_all(
        section_one(both_moved, cos_seq, sin_seq, total_items, columns_each),
        "seq",
        split_axis=2,
        concat_axis=3,
        tiled=True,
    )
    z_real = spectra_rows[0]
    z_imag = spectra_rows[1]
    cos_outer, sin_outer = tables(BLOCK, BLOCK, BLOCK)
    cos_inner, sin_inner = tables(inner_len, inner_len, inner_len)
    cos_mid, sin_mid = tables(BLOCK, inner_len, tokens_here)
    global_item = seq_pos * item_count + lax.iota(jnp.int32, item_count)
    freq = global_item % doubled
    twiddle_grid = lax.iota(jnp.int32, tokens_here)[None, :] * freq[:, None] % padded_len
    twiddle_angle = twiddle_grid.astype(jnp.float32) * (two_pi / padded_len)
    cos_twiddle = jnp.cos(twiddle_angle)
    sin_twiddle = jnp.sin(twiddle_angle)
    z_real, z_imag = rotate(z_real, z_imag, cos_twiddle, sin_twiddle)
    family = z_real.shape[0]
    z_real = z_real.reshape(family, item_count, BLOCK, inner_len)
    z_imag = z_imag.reshape(family, item_count, BLOCK, inner_len)
    z_real, z_imag = dft_apply(z_real, z_imag, "fiab,ae->fieb", cos_outer, sin_outer)
    z_real, z_imag = rotate(z_real, z_imag, cos_mid, sin_mid)
    z_real, z_imag = dft_apply(z_real, z_imag, "fieb,bg->fieg", cos_inner, sin_inner)
    prod_real = z_real[0] * z_real[1] - z_imag[0] * z_imag[1]
    prod_imag = z_real[0] * z_imag[1] + z_imag[0] * z_real[1]
    prod_real, prod_imag = dft_apply(prod_real, prod_imag, "ieg,gb->ieb", cos_inner, -sin_inner)
    prod_real, prod_imag = rotate(prod_real, prod_imag, cos_mid, -sin_mid)
    prod_real, prod_imag = dft_apply(prod_real, prod_imag, "ieb,ea->iab", cos_outer, -sin_outer)
    prod_real = prod_real.reshape(item_count, tokens_here)
    prod_imag = prod_imag.reshape(item_count, tokens_here)
    prod_real, prod_imag = rotate(prod_real, prod_imag, cos_twiddle, -sin_twiddle)
    returned = lax.all_to_all(
        jnp.stack([prod_real, prod_imag]), "seq", split_axis=2, concat_axis=1, tiled=True
    )
    returned = returned.reshape(2, channels, doubled, columns_each)
    partial_out = jnp.einsum("ckt,sk->cst", returned[0], cos_seq, precision=highest) - jnp.einsum(
        "ckt,sk->cst", returned[1], sin_seq, precision=highest
    )
    partial_out = partial_out * (1.0 / padded_len)
    longconv = lax.all_to_all(partial_out, "seq", split_axis=1, concat_axis=2, tiled=True).reshape(
        channels, tokens_here
    )
    gated = (queries * (longconv + skip_gain[:, None] * product)).astype(jnp.bfloat16)
    return lax.all_to_all(gated, "ch", split_axis=1, concat_axis=0, tiled=True)

MESH = pl.DeviceIdType.MESH


def owner_kernel(
    seq_count,
    ch_count,
    streams_in,
    filt_in,
    taps_hbm,
    gains_hbm,
    out,
    taps_in,
    gains_in,
    streams,
    filt,
    send_x,
    send_f,
    got_x,
    got_f,
    tap_rows,
    rows,
    lags,
    done,
    part,
    send_o,
    got_o,
    load_sem,
    x_send,
    x_recv,
    f_send,
    f_recv,
    o_send,
    o_recv,
):
    count = seq_count * ch_count
    seq_pos, ch_pos = lax.axis_index("seq"), lax.axis_index("ch")
    me = seq_pos * ch_count + ch_pos
    mine = ch_pos * seq_count + seq_pos
    width = streams.shape[2]
    span_f = filt.shape[1]
    tap_count = taps_in.shape[1]
    blocks = width * count // LANES
    half = blocks // 2
    base = 8 * blocks
    f32, bf16 = jnp.float32, jnp.bfloat16

    def peer(step):
        other = lax.rem(me + step, count)
        return other, other // ch_count, lax.rem(other, ch_count)

    barrier = pltpu.get_barrier_semaphore()

    @pl.loop(1, count)
    def _(step):
        _, s, c = peer(step)
        pl.semaphore_signal(barrier, inc=1, device_id=(s, c), device_id_type=MESH)

    load_f = pltpu.make_async_copy(filt_in, filt, load_sem.at[0])
    load_x = pltpu.make_async_copy(streams_in, streams, load_sem.at[1])
    load_x.start()
    load_f.start()
    load_t = pltpu.make_async_copy(taps_hbm, taps_in, load_sem.at[2])
    load_g = pltpu.make_async_copy(gains_hbm, gains_in, load_sem.at[3])
    load_t.start()
    load_g.start()
    load_x.wait()

    @pl.loop(0, streams.shape[1] // 16)
    def _(m):
        at = pl.ds(pl.multiple_of(16 * m, 16), 16)
        for i in range(3):
            values = streams[i, at, :].astype(f32)
            for e in range(4):
                send_x[4 * m + e, i] = values[4 * e : 4 * e + 4].astype(bf16)

    load_f.wait()
    for s in range(seq_count):
        send_f[s] = filt[GROUP * s : GROUP * (s + 1), :].astype(bf16)
    pl.semaphore_wait(barrier, count - 1)

    def filter_copy(s_to, s_from):
        at = pl.ds(pl.multiple_of(LANES + s_from * span_f, LANES), span_f)
        return pltpu.make_async_remote_copy(
            src_ref=send_f.at[s_to],
            dst_ref=got_f.at[:, at],
            send_sem=f_send.at[s_to],
            recv_sem=f_recv.at[s_from],
            device_id=(s_to, ch_pos),
            device_id_type=MESH,
        )

    def stream_copy(other, s, c, source):
        at = pl.ds(pl.multiple_of(LANES + source * width, LANES), width)
        block = c * seq_count + s
        return pltpu.make_async_remote_copy(
            src_ref=send_x.at[block],
            dst_ref=got_x.at[:, :, at],
            send_sem=x_send.at[other],
            recv_sem=x_recv.at[source],
            device_id=(s, c),
            device_id_type=MESH,
        )

    def out_copy(other, source):
        return pltpu.make_async_remote_copy(
            src_ref=send_o.at[other],
            dst_ref=got_o.at[source],
            send_sem=o_send.at[other],
            recv_sem=o_recv.at[source],
            device_id=(other // ch_count, lax.rem(other, ch_count)),
            device_id_type=MESH,
        )

    @pl.loop(1, seq_count)
    def _(step):
        filter_copy(lax.rem(seq_pos + step, seq_count), seq_pos).start()

    @pl.loop(1, count)
    def _(step):
        other, s, c = peer(step)
        stream_copy(other, s, c, me).start()

    load_t.wait()
    load_g.wait()
    lane = lax.broadcasted_iota(jnp.int32, (tap_count, LANES), 1)
    for c in range(GROUP):
        for i in range(3):
            column = jnp.sum(jnp.where(lane == GROUP * mine + c, taps_in[i], 0.0), axis=1, keepdims=True)
            tap_rows[pl.ds(32 * i + c, tap_count, stride=GROUP), :] = jnp.broadcast_to(column, (tap_count, LANES))
    rows[0:base, :] = jnp.zeros((base, LANES), f32)
    for i in range(3):
        got_x[i, :, 0:LANES] = jnp.zeros((GROUP, LANES), bf16)
    got_f[:, 0:LANES] = jnp.zeros((GROUP, LANES), bf16)

    got_f[:, pl.ds(pl.multiple_of(LANES + seq_pos * span_f, LANES), span_f)] = send_f[seq_pos]
    for i in range(3):
        got_x[i, :, pl.ds(pl.multiple_of(LANES + me * width, LANES), width)] = send_x[mine, i]

    @pl.loop(1, seq_count)
    def _(step):
        source = lax.rem(seq_pos + step, seq_count)
        filter_copy(source, source).wait_recv()

    row_at = lax.broadcasted_iota(jnp.int32, (LANES, LANES), 0)
    lane_at = lax.broadcasted_iota(jnp.int32, (LANES, LANES), 1)
    upper = lane_at >= row_at

    @pl.loop(0, blocks // SPAN)
    def _(big):
        wide = SPAN * LANES
        window = got_f[:, pl.ds(pl.multiple_of(big * wide, LANES), wide + LANES)].astype(f32)
        for c in range(GROUP):
            last = None
            for u in range(SPAN + 1):
                h = jnp.broadcast_to(window[c : c + 1, LANES * u : LANES * (u + 1)], (LANES, LANES))
                turn = pltpu.roll(h, 0, 1, stride=1, stride_axis=0)
                if u > 0:
                    at = pl.ds(pl.multiple_of((big * SPAN + u - 1) * LANES, LANES), LANES)
                    lags[c, at, :] = jnp.where(upper, turn, last).astype(bf16)
                last = turn

    chunk = 4 * LANES
    taps = []
    for j in range(tap_count):
        r = [tap_rows[32 * i + GROUP * j : 32 * i + GROUP * j + GROUP, :] for i in range(3)]
        qk = jnp.concatenate(r[:2], axis=0)
        taps.append([jnp.concatenate([t] * 4, axis=1) for t in (qk, r[2])])

    pairs = count // 2
    start = me // 2

    def arrived(source, needed):
        @pl.when(needed & (source != me))
        def _():
            stream_copy(source, source // ch_count, lax.rem(source, ch_count), source).wait_recv()

    arrived(2 * start + 1, True)

    @pl.loop(0, pairs)
    def _(turn):
        n = lax.rem(start - turn + pairs, pairs)
        arrived(2 * n, True)
        arrived(lax.rem(2 * n - 1 + count, count), turn < pairs - 1)

        at = pl.ds(pl.multiple_of(n * chunk, LANES), chunk + LANES)
        q, k, v = [got_x[i, :, at].astype(f32) for i in range(3)]
        shorts = []
        for which, ext in enumerate((jnp.concatenate([q, k], axis=0), v)):
            total = taps[0][which] * ext[:, LANES:]
            for j in range(1, tap_count):
                total = total + taps[j][which] * pltpu.roll(ext, j, 1)[:, LANES:]
            shorts.append(total.astype(bf16).astype(f32))
        product = shorts[0][GROUP:] * shorts[1]
        both = jnp.concatenate([product, shorts[0][:GROUP]], axis=0)
        for u in range(4):
            rows[pl.ds(pl.multiple_of(base + 8 * (4 * n + u), 8), 8), :] = both[:, LANES * u : LANES * (u + 1)]

    gain_lane = lax.broadcasted_iota(jnp.int32, gains_in.shape, 1)

    def partial_conv(c, first, many, d_from):
        at = [pl.ds(base + c + 8 * (first - d), many, stride=8) for d in range(d_from, d_from + half)]
        shifted = jnp.concatenate([rows[a, :].astype(bf16) for a in at], axis=1)
        return jnp.dot(shifted, lags[c, LANES * d_from : LANES * (d_from + half), :], preferred_element_type=f32)

    def finish(c, first, conv):
        product = rows[pl.ds(base + 8 * first + c, half, stride=8), :]
        q = rows[pl.ds(base + 8 * first + GROUP + c, half, stride=8), :]
        gain = jnp.sum(jnp.where(gain_lane == GROUP * seq_pos + c, gains_in[...], 0.0), axis=1, keepdims=True)
        done[pl.ds(GROUP * first + c, half, stride=GROUP), :] = q * (conv + gain * product)

    def send_half(first):
        for t in range(first, first + count // 2):
            send_o[t] = done[8 * t : 8 * t + 8, :].astype(bf16)

        @pl.loop(0, count // 2)
        def _(step):
            other = first + lax.rem(me + step, count // 2)

            @pl.when(other != me)
            def _():
                out_copy(other, mine).start()

    for c in range(GROUP):
        conv = partial_conv(c, 0, blocks, 0)
        finish(c, 0, conv[:half])
        part[c] = conv[half:]
    send_half(0)
    for c in range(GROUP):
        finish(c, half, part[c] + partial_conv(c, half, half, half))
    send_half(count // 2)

    got_o[mine] = send_o[me]

    @pl.loop(1, seq_count)
    def _(step):
        filter_copy(lax.rem(seq_pos + step, seq_count), seq_pos).wait_send()

    @pl.loop(1, count)
    def _(step):
        other, s, c = peer(step)
        stream_copy(other, s, c, me).wait_send()

    @pl.loop(1, count)
    def _(step):
        other, s, c = peer(step)
        out_copy(other, c * seq_count + s).wait_recv()

    @pl.loop(0, count // 4)
    def _(m):
        parts = [got_o[4 * m + e].astype(f32) for e in range(4)]
        at = pl.ds(pl.multiple_of(16 * m, 16), 16)
        for side in range(2):
            piece = jnp.concatenate([p[4 * side : 4 * side + 4] for p in parts], axis=0)
            out[at, LANES * side : LANES * (side + 1)] = piece.astype(bf16)

    @pl.loop(1, count)
    def _(step):
        out_copy(lax.rem(me + step, count), mine).wait_send()


def owner_local(streams, conv_taps, long_filter, skip_gain):
    seq_count, ch_count = lax.axis_size("seq"), lax.axis_size("ch")
    count = seq_count * ch_count
    channels, width = streams.shape[1:]
    length = width * count
    blocks = length // LANES
    dma = pltpu.SemaphoreType.DMA
    f32, bf16 = jnp.float32, jnp.bfloat16
    anywhere = pl.BlockSpec(memory_space=pltpu.MemorySpace.HBM)
    inside = pl.BlockSpec(memory_space=pltpu.VMEM)
    return pl.pallas_call(
        functools.partial(owner_kernel, seq_count, ch_count),
        out_shape=jax.ShapeDtypeStruct((channels, width), bf16),
        in_specs=[anywhere] * 4,
        out_specs=inside,
        scratch_shapes=[
            pltpu.VMEM((3, conv_taps.shape[2], channels), f32),
            pltpu.VMEM((1, skip_gain.shape[0]), f32),
            pltpu.VMEM(streams.shape, bf16),
            pltpu.VMEM(long_filter.shape, f32),
            pltpu.VMEM((count, 3, GROUP, width), bf16),
            pltpu.VMEM((seq_count, GROUP, long_filter.shape[1]), bf16),
            pltpu.VMEM((3, GROUP, LANES + length), bf16),
            pltpu.VMEM((GROUP, LANES + length), bf16),
            pltpu.VMEM((96, LANES), f32),
            pltpu.VMEM((16 * blocks, LANES), f32),
            pltpu.VMEM((GROUP, length, LANES), bf16),
            pltpu.VMEM((GROUP * blocks, LANES), f32),
            pltpu.VMEM((GROUP, blocks // 2, LANES), f32),
            pltpu.VMEM((count, 8, LANES), bf16),
            pltpu.VMEM((count, 8, LANES), bf16),
            dma((4,)),
            dma((count,)),
            dma((count,)),
            dma((seq_count,)),
            dma((seq_count,)),
            dma((count,)),
            dma((count,)),
        ],
        compiler_params=pltpu.CompilerParams(
            collective_id=0, has_side_effects=True, vmem_limit_bytes=48 * 1024 * 1024
        ),
    )(streams, long_filter, jnp.swapaxes(conv_taps, 1, 2), skip_gain[None, :])


def pick(streams, conv_taps, long_filter, skip_gain):
    count = lax.axis_size("seq") * lax.axis_size("ch")
    tap_fit = conv_taps.shape[2] <= 8
    tokens_fit = streams.shape[2] == 2 * LANES and streams.shape[1] == LANES
    fits = streams.shape[1] == GROUP * count and tokens_fit and tap_fit
    return (owner_local if fits else local)(streams, conv_taps, long_filter, skip_gain)


def solution(mesh):
    return jax.shard_map(
        pick,
        mesh=mesh,
        in_specs=(P(None, None, ("seq", "ch")), P(), P("ch", "seq"), P("ch")),
        out_specs=P(None, ("seq", "ch")),
        check_vma=False,
    )
```

```python
import functools
import math

import jax
import jax.numpy as jnp
from jax import lax
from jax.experimental import pallas as pl
from jax.experimental.pallas import tpu as pltpu
from jax.sharding import PartitionSpec as P

BLOCK = 64
LANES = 128
GROUP = 4
SPAN = 8


highest = lax.Precision.HIGHEST
two_pi = 2.0 * math.pi


def from_behind(value, axis, steps):
    count = lax.axis_size(axis)
    initial, last = (max(0, -steps), min(count, count - steps))
    return lax.ppermute(value, axis, [(source, source + steps) for source in range(initial, last)])


def tables(row_count, col_count, period):
    grid = lax.broadcasted_iota(jnp.int32, (row_count, col_count), 0) * lax.broadcasted_iota(
        jnp.int32, (row_count, col_count), 1
    )
    angle = (grid % period).astype(jnp.float32) * (two_pi / period)
    return (jnp.cos(angle), jnp.sin(angle))


def short_filter(block_in, upstream, weights):
    tap_count = weights.shape[2]
    extended = jnp.concatenate([upstream, block_in], axis=2).astype(jnp.float32)
    length_here = block_in.shape[2]
    summed = jnp.zeros(block_in.shape, jnp.float32)
    for offset in range(tap_count):
        begin = tap_count - 1 - offset
        summed = (
            summed
            + weights[:, :, offset : offset + 1] * extended[:, :, begin : begin + length_here]
        )
    return summed.astype(jnp.bfloat16)


def rotate(real_part, imag_part, cosine, sine):
    return (real_part * cosine + imag_part * sine, imag_part * cosine - real_part * sine)


def dft_apply(real_part, imag_part, form, cosine, sine):
    first = jnp.einsum(form, real_part, cosine, precision=highest) + jnp.einsum(
        form, imag_part, sine, precision=highest
    )
    second = jnp.einsum(form, imag_part, cosine, precision=highest) - jnp.einsum(
        form, real_part, sine, precision=highest
    )
    return (first, second)


def section_one(moved, cos_seq, sin_seq, total_items, columns_each):
    family = moved.shape[0]
    real_part = jnp.einsum("fcst,sk->fckt", moved, cos_seq, precision=highest)
    imag_part = -jnp.einsum("fcst,sk->fckt", moved, sin_seq, precision=highest)
    return jnp.stack([real_part, imag_part]).reshape(2, family, total_items, columns_each)


def local(streams, conv_taps, long_filter, skip_gain):
    seq_count = lax.axis_size("seq")
    seq_pos = lax.axis_index("seq")
    group_pos = lax.axis_index("ch")
    channels = long_filter.shape[0]
    tokens_here = long_filter.shape[1]
    tap_count = conv_taps.shape[2]
    length = tokens_here * seq_count
    padded_len = 2 * length
    columns_each = tokens_here // seq_count
    doubled = 2 * seq_count
    item_count = channels * doubled // seq_count
    total_items = channels * doubled
    inner_len = tokens_here // BLOCK
    cos_seq, sin_seq = tables(seq_count, doubled, doubled)
    regrouped = lax.all_to_all(streams, "ch", split_axis=1, concat_axis=2, tiled=True)
    upstream = from_behind(regrouped[:, :, regrouped.shape[2] - (tap_count - 1) :], "seq", 1)
    own_taps = lax.dynamic_slice_in_dim(conv_taps, group_pos * channels, channels, 1)
    shorts = short_filter(regrouped, upstream, own_taps)
    queries = shorts[0].astype(jnp.float32)
    product = shorts[1].astype(jnp.float32) * shorts[2].astype(jnp.float32)
    both_moved = lax.all_to_all(
        jnp.stack([product, long_filter]).reshape(2, channels, 1, tokens_here),
        "seq",
        split_axis=3,
        concat_axis=2,
        tiled=True,
    )
    spectra_rows = lax.all_to_all(
        section_one(both_moved, cos_seq, sin_seq, total_items, columns_each),
        "seq",
        split_axis=2,
        concat_axis=3,
        tiled=True,
    )
    z_real = spectra_rows[0]
    z_imag = spectra_rows[1]
    cos_outer, sin_outer = tables(BLOCK, BLOCK, BLOCK)
    cos_inner, sin_inner = tables(inner_len, inner_len, inner_len)
    cos_mid, sin_mid = tables(BLOCK, inner_len, tokens_here)
    global_item = seq_pos * item_count + lax.iota(jnp.int32, item_count)
    freq = global_item % doubled
    twiddle_grid = lax.iota(jnp.int32, tokens_here)[None, :] * freq[:, None] % padded_len
    twiddle_angle = twiddle_grid.astype(jnp.float32) * (two_pi / padded_len)
    cos_twiddle = jnp.cos(twiddle_angle)
    sin_twiddle = jnp.sin(twiddle_angle)
    z_real, z_imag = rotate(z_real, z_imag, cos_twiddle, sin_twiddle)
    family = z_real.shape[0]
    z_real = z_real.reshape(family, item_count, BLOCK, inner_len)
    z_imag = z_imag.reshape(family, item_count, BLOCK, inner_len)
    z_real, z_imag = dft_apply(z_real, z_imag, "fiab,ae->fieb", cos_outer, sin_outer)
    z_real, z_imag = rotate(z_real, z_imag, cos_mid, sin_mid)
    z_real, z_imag = dft_apply(z_real, z_imag, "fieb,bg->fieg", cos_inner, sin_inner)
    prod_real = z_real[0] * z_real[1] - z_imag[0] * z_imag[1]
    prod_imag = z_real[0] * z_imag[1] + z_imag[0] * z_real[1]
    prod_real, prod_imag = dft_apply(prod_real, prod_imag, "ieg,gb->ieb", cos_inner, -sin_inner)
    prod_real, prod_imag = rotate(prod_real, prod_imag, cos_mid, -sin_mid)
    prod_real, prod_imag = dft_apply(prod_real, prod_imag, "ieb,ea->iab", cos_outer, -sin_outer)
    prod_real = prod_real.reshape(item_count, tokens_here)
    prod_imag = prod_imag.reshape(item_count, tokens_here)
    prod_real, prod_imag = rotate(prod_real, prod_imag, cos_twiddle, -sin_twiddle)
    returned = lax.all_to_all(
        jnp.stack([prod_real, prod_imag]), "seq", split_axis=2, concat_axis=1, tiled=True
    )
    returned = returned.reshape(2, channels, doubled, columns_each)
    partial_out = jnp.einsum("ckt,sk->cst", returned[0], cos_seq, precision=highest) - jnp.einsum(
        "ckt,sk->cst", returned[1], sin_seq, precision=highest
    )
    partial_out = partial_out * (1.0 / padded_len)
    longconv = lax.all_to_all(partial_out, "seq", split_axis=1, concat_axis=2, tiled=True).reshape(
        channels, tokens_here
    )
    gated = (queries * (longconv + skip_gain[:, None] * product)).astype(jnp.bfloat16)
    return lax.all_to_all(gated, "ch", split_axis=1, concat_axis=0, tiled=True)

MESH = pl.DeviceIdType.MESH


def owner_kernel(
    seq_count,
    ch_count,
    streams_in,
    filt_in,
    taps_hbm,
    gains_hbm,
    out,
    taps_in,
    gains_in,
    streams,
    filt,
    send_x,
    send_f,
    got_x,
    got_f,
    tap_rows,
    rows,
    lags,
    done,
    part,
    send_o,
    got_o,
    load_sem,
    x_send,
    x_recv,
    f_send,
    f_recv,
    o_send,
    o_recv,
):
    count = seq_count * ch_count
    seq_pos, ch_pos = lax.axis_index("seq"), lax.axis_index("ch")
    me = seq_pos * ch_count + ch_pos
    mine = ch_pos * seq_count + seq_pos
    width = streams.shape[2]
    span_f = filt.shape[1]
    tap_count = taps_in.shape[1]
    blocks = width * count // LANES
    half = blocks // 2
    base = 8 * blocks
    f32, bf16 = jnp.float32, jnp.bfloat16

    def peer(step):
        other = lax.rem(me + step, count)
        return other, other // ch_count, lax.rem(other, ch_count)

    barrier = pltpu.get_barrier_semaphore()

    @pl.loop(1, count)
    def _(step):
        _, s, c = peer(step)
        pl.semaphore_signal(barrier, inc=1, device_id=(s, c), device_id_type=MESH)

    load_f = pltpu.make_async_copy(filt_in, filt, load_sem.at[0])
    load_x = pltpu.make_async_copy(streams_in, streams, load_sem.at[1])
    load_x.start()
    load_f.start()
    load_t = pltpu.make_async_copy(taps_hbm, taps_in, load_sem.at[2])
    load_g = pltpu.make_async_copy(gains_hbm, gains_in, load_sem.at[3])
    load_t.start()
    load_g.start()
    load_x.wait()

    @pl.loop(0, streams.shape[1] // 16)
    def _(m):
        at = pl.ds(pl.multiple_of(16 * m, 16), 16)
        for i in range(3):
            values = streams[i, at, :].astype(f32)
            for e in range(4):
                send_x[4 * m + e, i] = values[4 * e : 4 * e + 4].astype(bf16)

    load_f.wait()
    for s in range(seq_count):
        send_f[s] = filt[GROUP * s : GROUP * (s + 1), :].astype(bf16)
    pl.semaphore_wait(barrier, count - 1)

    def filter_copy(s_to, s_from):
        at = pl.ds(pl.multiple_of(LANES + s_from * span_f, LANES), span_f)
        return pltpu.make_async_remote_copy(
            src_ref=send_f.at[s_to],
            dst_ref=got_f.at[:, at],
            send_sem=f_send.at[s_to],
            recv_sem=f_recv.at[s_from],
            device_id=(s_to, ch_pos),
            device_id_type=MESH,
        )

    def stream_copy(other, s, c, source):
        at = pl.ds(pl.multiple_of(LANES + source * width, LANES), width)
        block = c * seq_count + s
        return pltpu.make_async_remote_copy(
            src_ref=send_x.at[block],
            dst_ref=got_x.at[:, :, at],
            send_sem=x_send.at[other],
            recv_sem=x_recv.at[source],
            device_id=(s, c),
            device_id_type=MESH,
        )

    def out_copy(other, source):
        return pltpu.make_async_remote_copy(
            src_ref=send_o.at[other],
            dst_ref=got_o.at[source],
            send_sem=o_send,
            recv_sem=o_recv,
            device_id=(other // ch_count, lax.rem(other, ch_count)),
            device_id_type=MESH,
        )

    @pl.loop(1, seq_count)
    def _(step):
        filter_copy(lax.rem(seq_pos + step, seq_count), seq_pos).start()

    @pl.loop(1, count)
    def _(step):
        other, s, c = peer(step)
        stream_copy(other, s, c, me).start()

    load_t.wait()
    load_g.wait()
    lane = lax.broadcasted_iota(jnp.int32, (tap_count, LANES), 1)
    for c in range(GROUP):
        for i in range(3):
            column = jnp.sum(jnp.where(lane == GROUP * mine + c, taps_in[i], 0.0), axis=1, keepdims=True)
            tap_rows[pl.ds(32 * i + c, tap_count, stride=GROUP), :] = jnp.broadcast_to(column, (tap_count, LANES))
    rows[0:base, :] = jnp.zeros((base, LANES), f32)
    for i in range(3):
        got_x[i, :, 0:LANES] = jnp.zeros((GROUP, LANES), bf16)
    got_f[:, 0:LANES] = jnp.zeros((GROUP, LANES), bf16)

    got_f[:, pl.ds(pl.multiple_of(LANES + seq_pos * span_f, LANES), span_f)] = send_f[seq_pos]
    for i in range(3):
        got_x[i, :, pl.ds(pl.multiple_of(LANES + me * width, LANES), width)] = send_x[mine, i]

    @pl.loop(1, seq_count)
    def _(step):
        source = lax.rem(seq_pos + step, seq_count)
        filter_copy(source, source).wait_recv()

    row_at = lax.broadcasted_iota(jnp.int32, (LANES, LANES), 0)
    lane_at = lax.broadcasted_iota(jnp.int32, (LANES, LANES), 1)
    upper = lane_at >= row_at

    @pl.loop(0, blocks // SPAN)
    def _(big):
        wide = SPAN * LANES
        window = got_f[:, pl.ds(pl.multiple_of(big * wide, LANES), wide + LANES)].astype(f32)
        for c in range(GROUP):
            last = None
            for u in range(SPAN + 1):
                h = jnp.broadcast_to(window[c : c + 1, LANES * u : LANES * (u + 1)], (LANES, LANES))
                turn = pltpu.roll(h, 0, 1, stride=1, stride_axis=0)
                if u > 0:
                    at = pl.ds(pl.multiple_of((big * SPAN + u - 1) * LANES, LANES), LANES)
                    lags[c, at, :] = jnp.where(upper, turn, last).astype(bf16)
                last = turn

    chunk = 4 * LANES
    taps = []
    for j in range(tap_count):
        r = [tap_rows[32 * i + GROUP * j : 32 * i + GROUP * j + GROUP, :] for i in range(3)]
        qk = jnp.concatenate(r[:2], axis=0)
        taps.append([jnp.concatenate([t] * 4, axis=1) for t in (qk, r[2])])

    pairs = count // 2
    start = me // 2

    def arrived(source, needed):
        @pl.when(needed & (source != me))
        def _():
            stream_copy(source, source // ch_count, lax.rem(source, ch_count), source).wait_recv()

    arrived(2 * start + 1, True)

    @pl.loop(0, pairs)
    def _(turn):
        n = lax.rem(start - turn + pairs, pairs)
        arrived(2 * n, True)
        arrived(lax.rem(2 * n - 1 + count, count), turn < pairs - 1)

        at = pl.ds(pl.multiple_of(n * chunk, LANES), chunk + LANES)
        q, k, v = [got_x[i, :, at].astype(f32) for i in range(3)]
        shorts = []
        for which, ext in enumerate((jnp.concatenate([q, k], axis=0), v)):
            total = taps[0][which] * ext[:, LANES:]
            for j in range(1, tap_count):
                total = total + taps[j][which] * pltpu.roll(ext, j, 1)[:, LANES:]
            shorts.append(total.astype(bf16).astype(f32))
        product = shorts[0][GROUP:] * shorts[1]
        both = jnp.concatenate([product, shorts[0][:GROUP]], axis=0)
        for u in range(4):
            rows[pl.ds(pl.multiple_of(base + 8 * (4 * n + u), 8), 8), :] = both[:, LANES * u : LANES * (u + 1)]

    gain_lane = lax.broadcasted_iota(jnp.int32, gains_in.shape, 1)

    def partial_conv(c, first, many, d_from):
        at = [pl.ds(base + c + 8 * (first - d), many, stride=8) for d in range(d_from, d_from + half)]
        shifted = jnp.concatenate([rows[a, :].astype(bf16) for a in at], axis=1)
        return jnp.dot(shifted, lags[c, LANES * d_from : LANES * (d_from + half), :], preferred_element_type=f32)

    def finish(c, first, conv):
        product = rows[pl.ds(base + 8 * first + c, half, stride=8), :]
        q = rows[pl.ds(base + 8 * first + GROUP + c, half, stride=8), :]
        gain = jnp.sum(jnp.where(gain_lane == GROUP * seq_pos + c, gains_in[...], 0.0), axis=1, keepdims=True)
        done[pl.ds(GROUP * first + c, half, stride=GROUP), :] = q * (conv + gain * product)

    def send_half(first):
        for t in range(first, first + count // 2):
            send_o[t] = done[8 * t : 8 * t + 8, :].astype(bf16)

        @pl.loop(0, count // 2)
        def _(step):
            other = first + lax.rem(me + step, count // 2)

            @pl.when(other != me)
            def _():
                out_copy(other, mine).start()

    for c in range(GROUP):
        conv = partial_conv(c, 0, blocks, 0)
        finish(c, 0, conv[:half])
        part[c] = conv[half:]
    send_half(0)
    for c in range(GROUP):
        finish(c, half, part[c] + partial_conv(c, half, half, half))
    send_half(count // 2)

    got_o[mine] = send_o[me]

    @pl.loop(1, seq_count)
    def _(step):
        filter_copy(lax.rem(seq_pos + step, seq_count), seq_pos).wait_send()

    @pl.loop(1, count)
    def _(step):
        other, s, c = peer(step)
        stream_copy(other, s, c, me).wait_send()

    others = pl.ds(0, count - 1)
    whole = pltpu.make_async_remote_copy(
        src_ref=send_o.at[others],
        dst_ref=got_o.at[others],
        send_sem=o_send,
        recv_sem=o_recv,
        device_id=(seq_pos, ch_pos),
        device_id_type=MESH,
    )
    whole.wait_recv()

    @pl.loop(0, count // 4)
    def _(m):
        parts = [got_o[4 * m + e].astype(f32) for e in range(4)]
        at = pl.ds(pl.multiple_of(16 * m, 16), 16)
        for side in range(2):
            piece = jnp.concatenate([p[4 * side : 4 * side + 4] for p in parts], axis=0)
            out[at, LANES * side : LANES * (side + 1)] = piece.astype(bf16)

    whole.wait_send()


def owner_local(streams, conv_taps, long_filter, skip_gain):
    seq_count, ch_count = lax.axis_size("seq"), lax.axis_size("ch")
    count = seq_count * ch_count
    channels, width = streams.shape[1:]
    length = width * count
    blocks = length // LANES
    dma = pltpu.SemaphoreType.DMA
    f32, bf16 = jnp.float32, jnp.bfloat16
    anywhere = pl.BlockSpec(memory_space=pltpu.MemorySpace.HBM)
    inside = pl.BlockSpec(memory_space=pltpu.VMEM)
    return pl.pallas_call(
        functools.partial(owner_kernel, seq_count, ch_count),
        out_shape=jax.ShapeDtypeStruct((channels, width), bf16),
        in_specs=[anywhere] * 4,
        out_specs=inside,
        scratch_shapes=[
            pltpu.VMEM((3, conv_taps.shape[2], channels), f32),
            pltpu.VMEM((1, skip_gain.shape[0]), f32),
            pltpu.VMEM(streams.shape, bf16),
            pltpu.VMEM(long_filter.shape, f32),
            pltpu.VMEM((count, 3, GROUP, width), bf16),
            pltpu.VMEM((seq_count, GROUP, long_filter.shape[1]), bf16),
            pltpu.VMEM((3, GROUP, LANES + length), bf16),
            pltpu.VMEM((GROUP, LANES + length), bf16),
            pltpu.VMEM((96, LANES), f32),
            pltpu.VMEM((16 * blocks, LANES), f32),
            pltpu.VMEM((GROUP, length, LANES), bf16),
            pltpu.VMEM((GROUP * blocks, LANES), f32),
            pltpu.VMEM((GROUP, blocks // 2, LANES), f32),
            pltpu.VMEM((count, 8, LANES), bf16),
            pltpu.VMEM((count, 8, LANES), bf16),
            dma((4,)),
            dma((count,)),
            dma((count,)),
            dma((seq_count,)),
            dma((seq_count,)),
            dma(()),
            dma(()),
        ],
        compiler_params=pltpu.CompilerParams(
            collective_id=0, has_side_effects=True, vmem_limit_bytes=48 * 1024 * 1024
        ),
    )(streams, long_filter, jnp.swapaxes(conv_taps, 1, 2), skip_gain[None, :])


def pick(streams, conv_taps, long_filter, skip_gain):
    count = lax.axis_size("seq") * lax.axis_size("ch")
    tap_fit = conv_taps.shape[2] <= 8
    tokens_fit = streams.shape[2] == 2 * LANES and streams.shape[1] == LANES
    fits = streams.shape[1] == GROUP * count and tokens_fit and tap_fit
    return (owner_local if fits else local)(streams, conv_taps, long_filter, skip_gain)


def solution(mesh):
    return jax.shard_map(
        pick,
        mesh=mesh,
        in_specs=(P(None, None, ("seq", "ch")), P(), P("ch", "seq"), P("ch")),
        out_specs=P(None, ("seq", "ch")),
        check_vma=False,
    )
```

```python
import functools
import math

import jax
import jax.numpy as jnp
from jax import lax
from jax.experimental import pallas as pl
from jax.experimental.pallas import tpu as pltpu
from jax.sharding import PartitionSpec as P

BLOCK = 64
LANES = 128
GROUP = 4
SPAN = 8


highest = lax.Precision.HIGHEST
two_pi = 2.0 * math.pi


def from_behind(value, axis, steps):
    count = lax.axis_size(axis)
    initial, last = (max(0, -steps), min(count, count - steps))
    return lax.ppermute(value, axis, [(source, source + steps) for source in range(initial, last)])


def tables(row_count, col_count, period):
    grid = lax.broadcasted_iota(jnp.int32, (row_count, col_count), 0) * lax.broadcasted_iota(
        jnp.int32, (row_count, col_count), 1
    )
    angle = (grid % period).astype(jnp.float32) * (two_pi / period)
    return (jnp.cos(angle), jnp.sin(angle))


def short_filter(block_in, upstream, weights):
    tap_count = weights.shape[2]
    extended = jnp.concatenate([upstream, block_in], axis=2).astype(jnp.float32)
    length_here = block_in.shape[2]
    summed = jnp.zeros(block_in.shape, jnp.float32)
    for offset in range(tap_count):
        begin = tap_count - 1 - offset
        summed = (
            summed
            + weights[:, :, offset : offset + 1] * extended[:, :, begin : begin + length_here]
        )
    return summed.astype(jnp.bfloat16)


def rotate(real_part, imag_part, cosine, sine):
    return (real_part * cosine + imag_part * sine, imag_part * cosine - real_part * sine)


def dft_apply(real_part, imag_part, form, cosine, sine):
    first = jnp.einsum(form, real_part, cosine, precision=highest) + jnp.einsum(
        form, imag_part, sine, precision=highest
    )
    second = jnp.einsum(form, imag_part, cosine, precision=highest) - jnp.einsum(
        form, real_part, sine, precision=highest
    )
    return (first, second)


def section_one(moved, cos_seq, sin_seq, total_items, columns_each):
    family = moved.shape[0]
    real_part = jnp.einsum("fcst,sk->fckt", moved, cos_seq, precision=highest)
    imag_part = -jnp.einsum("fcst,sk->fckt", moved, sin_seq, precision=highest)
    return jnp.stack([real_part, imag_part]).reshape(2, family, total_items, columns_each)


def local(streams, conv_taps, long_filter, skip_gain):
    seq_count = lax.axis_size("seq")
    seq_pos = lax.axis_index("seq")
    group_pos = lax.axis_index("ch")
    channels = long_filter.shape[0]
    tokens_here = long_filter.shape[1]
    tap_count = conv_taps.shape[2]
    length = tokens_here * seq_count
    padded_len = 2 * length
    columns_each = tokens_here // seq_count
    doubled = 2 * seq_count
    item_count = channels * doubled // seq_count
    total_items = channels * doubled
    inner_len = tokens_here // BLOCK
    cos_seq, sin_seq = tables(seq_count, doubled, doubled)
    regrouped = lax.all_to_all(streams, "ch", split_axis=1, concat_axis=2, tiled=True)
    upstream = from_behind(regrouped[:, :, regrouped.shape[2] - (tap_count - 1) :], "seq", 1)
    own_taps = lax.dynamic_slice_in_dim(conv_taps, group_pos * channels, channels, 1)
    shorts = short_filter(regrouped, upstream, own_taps)
    queries = shorts[0].astype(jnp.float32)
    product = shorts[1].astype(jnp.float32) * shorts[2].astype(jnp.float32)
    both_moved = lax.all_to_all(
        jnp.stack([product, long_filter]).reshape(2, channels, 1, tokens_here),
        "seq",
        split_axis=3,
        concat_axis=2,
        tiled=True,
    )
    spectra_rows = lax.all_to_all(
        section_one(both_moved, cos_seq, sin_seq, total_items, columns_each),
        "seq",
        split_axis=2,
        concat_axis=3,
        tiled=True,
    )
    z_real = spectra_rows[0]
    z_imag = spectra_rows[1]
    cos_outer, sin_outer = tables(BLOCK, BLOCK, BLOCK)
    cos_inner, sin_inner = tables(inner_len, inner_len, inner_len)
    cos_mid, sin_mid = tables(BLOCK, inner_len, tokens_here)
    global_item = seq_pos * item_count + lax.iota(jnp.int32, item_count)
    freq = global_item % doubled
    twiddle_grid = lax.iota(jnp.int32, tokens_here)[None, :] * freq[:, None] % padded_len
    twiddle_angle = twiddle_grid.astype(jnp.float32) * (two_pi / padded_len)
    cos_twiddle = jnp.cos(twiddle_angle)
    sin_twiddle = jnp.sin(twiddle_angle)
    z_real, z_imag = rotate(z_real, z_imag, cos_twiddle, sin_twiddle)
    family = z_real.shape[0]
    z_real = z_real.reshape(family, item_count, BLOCK, inner_len)
    z_imag = z_imag.reshape(family, item_count, BLOCK, inner_len)
    z_real, z_imag = dft_apply(z_real, z_imag, "fiab,ae->fieb", cos_outer, sin_outer)
    z_real, z_imag = rotate(z_real, z_imag, cos_mid, sin_mid)
    z_real, z_imag = dft_apply(z_real, z_imag, "fieb,bg->fieg", cos_inner, sin_inner)
    prod_real = z_real[0] * z_real[1] - z_imag[0] * z_imag[1]
    prod_imag = z_real[0] * z_imag[1] + z_imag[0] * z_real[1]
    prod_real, prod_imag = dft_apply(prod_real, prod_imag, "ieg,gb->ieb", cos_inner, -sin_inner)
    prod_real, prod_imag = rotate(prod_real, prod_imag, cos_mid, -sin_mid)
    prod_real, prod_imag = dft_apply(prod_real, prod_imag, "ieb,ea->iab", cos_outer, -sin_outer)
    prod_real = prod_real.reshape(item_count, tokens_here)
    prod_imag = prod_imag.reshape(item_count, tokens_here)
    prod_real, prod_imag = rotate(prod_real, prod_imag, cos_twiddle, -sin_twiddle)
    returned = lax.all_to_all(
        jnp.stack([prod_real, prod_imag]), "seq", split_axis=2, concat_axis=1, tiled=True
    )
    returned = returned.reshape(2, channels, doubled, columns_each)
    partial_out = jnp.einsum("ckt,sk->cst", returned[0], cos_seq, precision=highest) - jnp.einsum(
        "ckt,sk->cst", returned[1], sin_seq, precision=highest
    )
    partial_out = partial_out * (1.0 / padded_len)
    longconv = lax.all_to_all(partial_out, "seq", split_axis=1, concat_axis=2, tiled=True).reshape(
        channels, tokens_here
    )
    gated = (queries * (longconv + skip_gain[:, None] * product)).astype(jnp.bfloat16)
    return lax.all_to_all(gated, "ch", split_axis=1, concat_axis=0, tiled=True)

MESH = pl.DeviceIdType.MESH


def owner_kernel(
    seq_count,
    ch_count,
    streams_in,
    filt_in,
    taps_hbm,
    gains_hbm,
    out,
    taps_in,
    gains_in,
    streams,
    filt,
    send_x,
    send_f,
    got_x,
    got_f,
    tap_rows,
    rows,
    lags,
    done,
    part,
    send_o,
    got_o,
    load_sem,
    x_send,
    x_recv,
    f_send,
    f_recv,
    o_send,
    o_recv,
):
    count = seq_count * ch_count
    seq_pos, ch_pos = lax.axis_index("seq"), lax.axis_index("ch")
    me = seq_pos * ch_count + ch_pos
    mine = ch_pos * seq_count + seq_pos
    width = streams.shape[2]
    span_f = filt.shape[1]
    tap_count = taps_in.shape[1]
    blocks = width * count // LANES
    half = blocks // 2
    base = 8 * blocks
    f32, bf16 = jnp.float32, jnp.bfloat16

    def peer(step):
        other = lax.rem(me + step, count)
        return other, other // ch_count, lax.rem(other, ch_count)

    barrier = pltpu.get_barrier_semaphore()

    @pl.loop(1, count)
    def _(step):
        _, s, c = peer(step)
        pl.semaphore_signal(barrier, inc=1, device_id=(s, c), device_id_type=MESH)

    load_f = pltpu.make_async_copy(filt_in, filt, load_sem.at[0])
    load_x = pltpu.make_async_copy(streams_in, streams, load_sem.at[1])
    load_x.start()
    load_f.start()
    load_t = pltpu.make_async_copy(taps_hbm, taps_in, load_sem.at[2])
    load_g = pltpu.make_async_copy(gains_hbm, gains_in, load_sem.at[3])
    load_t.start()
    load_g.start()
    load_x.wait()

    @pl.loop(0, streams.shape[1] // 16)
    def _(m):
        at = pl.ds(pl.multiple_of(16 * m, 16), 16)
        for i in range(3):
            values = streams[i, at, :].astype(f32)
            for e in range(4):
                send_x[4 * m + e, i] = values[4 * e : 4 * e + 4].astype(bf16)

    load_f.wait()
    for s in range(seq_count):
        send_f[s] = filt[GROUP * s : GROUP * (s + 1), :].astype(bf16)
    pl.semaphore_wait(barrier, count - 1)

    def filter_copy(s_to, s_from):
        at = pl.ds(pl.multiple_of(LANES + s_from * span_f, LANES), span_f)
        return pltpu.make_async_remote_copy(
            src_ref=send_f.at[s_to],
            dst_ref=got_f.at[:, at],
            send_sem=f_send,
            recv_sem=f_recv,
            device_id=(s_to, ch_pos),
            device_id_type=MESH,
        )

    def stream_copy(other, s, c, source):
        at = pl.ds(pl.multiple_of(LANES + source * width, LANES), width)
        block = c * seq_count + s
        return pltpu.make_async_remote_copy(
            src_ref=send_x.at[block],
            dst_ref=got_x.at[:, :, at],
            send_sem=x_send,
            recv_sem=x_recv.at[source],
            device_id=(s, c),
            device_id_type=MESH,
        )

    def out_copy(other, source):
        return pltpu.make_async_remote_copy(
            src_ref=send_o.at[other],
            dst_ref=got_o.at[source],
            send_sem=o_send,
            recv_sem=o_recv,
            device_id=(other // ch_count, lax.rem(other, ch_count)),
            device_id_type=MESH,
        )

    @pl.loop(1, seq_count)
    def _(step):
        filter_copy(lax.rem(seq_pos + step, seq_count), seq_pos).start()

    @pl.loop(1, count)
    def _(step):
        other, s, c = peer(step)
        stream_copy(other, s, c, me).start()

    load_t.wait()
    load_g.wait()
    lane = lax.broadcasted_iota(jnp.int32, (tap_count, LANES), 1)
    for c in range(GROUP):
        for i in range(3):
            column = jnp.sum(jnp.where(lane == GROUP * mine + c, taps_in[i], 0.0), axis=1, keepdims=True)
            tap_rows[pl.ds(32 * i + c, tap_count, stride=GROUP), :] = jnp.broadcast_to(column, (tap_count, LANES))
    rows[0:base, :] = jnp.zeros((base, LANES), f32)
    for i in range(3):
        got_x[i, :, 0:LANES] = jnp.zeros((GROUP, LANES), bf16)
    got_f[:, 0:LANES] = jnp.zeros((GROUP, LANES), bf16)

    got_f[:, pl.ds(pl.multiple_of(LANES + seq_pos * span_f, LANES), span_f)] = send_f[seq_pos]
    for i in range(3):
        got_x[i, :, pl.ds(pl.multiple_of(LANES + me * width, LANES), width)] = send_x[mine, i]

    slots = pl.ds(0, seq_count - 1)
    filters = pltpu.make_async_remote_copy(
        src_ref=send_f.at[slots],
        dst_ref=send_f.at[slots],
        send_sem=f_send,
        recv_sem=f_recv,
        device_id=(seq_pos, ch_pos),
        device_id_type=MESH,
    )
    filters.wait_recv()

    row_at = lax.broadcasted_iota(jnp.int32, (LANES, LANES), 0)
    lane_at = lax.broadcasted_iota(jnp.int32, (LANES, LANES), 1)
    upper = lane_at >= row_at

    @pl.loop(0, blocks // SPAN)
    def _(big):
        wide = SPAN * LANES
        window = got_f[:, pl.ds(pl.multiple_of(big * wide, LANES), wide + LANES)].astype(f32)
        for c in range(GROUP):
            last = None
            for u in range(SPAN + 1):
                h = jnp.broadcast_to(window[c : c + 1, LANES * u : LANES * (u + 1)], (LANES, LANES))
                turn = pltpu.roll(h, 0, 1, stride=1, stride_axis=0)
                if u > 0:
                    at = pl.ds(pl.multiple_of((big * SPAN + u - 1) * LANES, LANES), LANES)
                    lags[c, at, :] = jnp.where(upper, turn, last).astype(bf16)
                last = turn

    chunk = 4 * LANES
    taps = []
    for j in range(tap_count):
        r = [tap_rows[32 * i + GROUP * j : 32 * i + GROUP * j + GROUP, :] for i in range(3)]
        qk = jnp.concatenate(r[:2], axis=0)
        taps.append([jnp.concatenate([t] * 4, axis=1) for t in (qk, r[2])])

    pairs = count // 2
    start = me // 2

    def arrived(source, needed):
        @pl.when(needed & (source != me))
        def _():
            stream_copy(source, source // ch_count, lax.rem(source, ch_count), source).wait_recv()

    arrived(2 * start + 1, True)

    @pl.loop(0, pairs)
    def _(turn):
        n = lax.rem(start - turn + pairs, pairs)
        arrived(2 * n, True)
        arrived(lax.rem(2 * n - 1 + count, count), turn < pairs - 1)

        at = pl.ds(pl.multiple_of(n * chunk, LANES), chunk + LANES)
        q, k, v = [got_x[i, :, at].astype(f32) for i in range(3)]
        shorts = []
        for which, ext in enumerate((jnp.concatenate([q, k], axis=0), v)):
            total = taps[0][which] * ext[:, LANES:]
            for j in range(1, tap_count):
                total = total + taps[j][which] * pltpu.roll(ext, j, 1)[:, LANES:]
            shorts.append(total.astype(bf16).astype(f32))
        product = shorts[0][GROUP:] * shorts[1]
        both = jnp.concatenate([product, shorts[0][:GROUP]], axis=0)
        for u in range(4):
            rows[pl.ds(pl.multiple_of(base + 8 * (4 * n + u), 8), 8), :] = both[:, LANES * u : LANES * (u + 1)]

    gain_lane = lax.broadcasted_iota(jnp.int32, gains_in.shape, 1)

    def partial_conv(c, first, many, d_from):
        at = [pl.ds(base + c + 8 * (first - d), many, stride=8) for d in range(d_from, d_from + half)]
        shifted = jnp.concatenate([rows[a, :].astype(bf16) for a in at], axis=1)
        return jnp.dot(shifted, lags[c, LANES * d_from : LANES * (d_from + half), :], preferred_element_type=f32)

    def finish(c, first, conv):
        product = rows[pl.ds(base + 8 * first + c, half, stride=8), :]
        q = rows[pl.ds(base + 8 * first + GROUP + c, half, stride=8), :]
        gain = jnp.sum(jnp.where(gain_lane == GROUP * seq_pos + c, gains_in[...], 0.0), axis=1, keepdims=True)
        done[pl.ds(GROUP * first + c, half, stride=GROUP), :] = q * (conv + gain * product)

    def send_half(first):
        for t in range(first, first + count // 2):
            send_o[t] = done[8 * t : 8 * t + 8, :].astype(bf16)

        @pl.loop(0, count // 2)
        def _(step):
            other = first + lax.rem(me + step, count // 2)

            @pl.when(other != me)
            def _():
                out_copy(other, mine).start()

    for c in range(GROUP):
        conv = partial_conv(c, 0, blocks, 0)
        finish(c, 0, conv[:half])
        part[c] = conv[half:]
    send_half(0)
    for c in range(GROUP):
        finish(c, half, part[c] + partial_conv(c, half, half, half))
    send_half(count // 2)

    got_o[mine] = send_o[me]

    others = pl.ds(0, count - 1)
    filters.wait_send()
    pltpu.make_async_remote_copy(
        src_ref=send_x.at[others],
        dst_ref=send_x.at[others],
        send_sem=x_send,
        recv_sem=x_recv.at[me],
        device_id=(seq_pos, ch_pos),
        device_id_type=MESH,
    ).wait_send()
    whole = pltpu.make_async_remote_copy(
        src_ref=send_o.at[others],
        dst_ref=got_o.at[others],
        send_sem=o_send,
        recv_sem=o_recv,
        device_id=(seq_pos, ch_pos),
        device_id_type=MESH,
    )
    whole.wait_recv()

    @pl.loop(0, count // 4)
    def _(m):
        parts = [got_o[4 * m + e].astype(f32) for e in range(4)]
        at = pl.ds(pl.multiple_of(16 * m, 16), 16)
        for side in range(2):
            piece = jnp.concatenate([p[4 * side : 4 * side + 4] for p in parts], axis=0)
            out[at, LANES * side : LANES * (side + 1)] = piece.astype(bf16)

    whole.wait_send()


def owner_local(streams, conv_taps, long_filter, skip_gain):
    seq_count, ch_count = lax.axis_size("seq"), lax.axis_size("ch")
    count = seq_count * ch_count
    channels, width = streams.shape[1:]
    length = width * count
    blocks = length // LANES
    dma = pltpu.SemaphoreType.DMA
    f32, bf16 = jnp.float32, jnp.bfloat16
    anywhere = pl.BlockSpec(memory_space=pltpu.MemorySpace.HBM)
    inside = pl.BlockSpec(memory_space=pltpu.VMEM)
    return pl.pallas_call(
        functools.partial(owner_kernel, seq_count, ch_count),
        out_shape=jax.ShapeDtypeStruct((channels, width), bf16),
        in_specs=[anywhere] * 4,
        out_specs=inside,
        scratch_shapes=[
            pltpu.VMEM((3, conv_taps.shape[2], channels), f32),
            pltpu.VMEM((1, skip_gain.shape[0]), f32),
            pltpu.VMEM(streams.shape, bf16),
            pltpu.VMEM(long_filter.shape, f32),
            pltpu.VMEM((count, 3, GROUP, width), bf16),
            pltpu.VMEM((seq_count, GROUP, long_filter.shape[1]), bf16),
            pltpu.VMEM((3, GROUP, LANES + length), bf16),
            pltpu.VMEM((GROUP, LANES + length), bf16),
            pltpu.VMEM((96, LANES), f32),
            pltpu.VMEM((16 * blocks, LANES), f32),
            pltpu.VMEM((GROUP, length, LANES), bf16),
            pltpu.VMEM((GROUP * blocks, LANES), f32),
            pltpu.VMEM((GROUP, blocks // 2, LANES), f32),
            pltpu.VMEM((count, 8, LANES), bf16),
            pltpu.VMEM((count, 8, LANES), bf16),
            dma((4,)),
            dma(()),
            dma((count,)),
            dma(()),
            dma(()),
            dma(()),
            dma(()),
        ],
        compiler_params=pltpu.CompilerParams(
            collective_id=0, has_side_effects=True, vmem_limit_bytes=48 * 1024 * 1024
        ),
    )(streams, long_filter, jnp.swapaxes(conv_taps, 1, 2), skip_gain[None, :])


def pick(streams, conv_taps, long_filter, skip_gain):
    count = lax.axis_size("seq") * lax.axis_size("ch")
    tap_fit = conv_taps.shape[2] <= 8
    tokens_fit = streams.shape[2] == 2 * LANES and streams.shape[1] == LANES
    fits = streams.shape[1] == GROUP * count and tokens_fit and tap_fit
    return (owner_local if fits else local)(streams, conv_taps, long_filter, skip_gain)


def solution(mesh):
    return jax.shard_map(
        pick,
        mesh=mesh,
        in_specs=(P(None, None, ("seq", "ch")), P(), P("ch", "seq"), P("ch")),
        out_specs=P(None, ("seq", "ch")),
        check_vma=False,
    )
```
